32 devices in a mesh: seq: 16 (over z, y, x), head: 2 (over core).
Axes of the slice: x: 2, y: 2, z: 4, core: 2. Of those that a mesh axis runs over, the one named last changes fastest.
Arguments:
- block_input: bfloat16 [4096, 1024], P('seq'), may hold values from -6 to 6
- seq_pieces: int32 [5], replicated, may hold values from 1 to 4, as said below
- norm_gain: float32 [1024], replicated, may hold values from 0.5 to 1.5
- w_zx: bfloat16 [1024, 2, 2048], P(None, None, 'head'), may hold values from -0.1875 to 0.1875
- w_bc: bfloat16 [1024, 256], P(None, 'head'), may hold values from -0.1875 to 0.1875
- w_dt: bfloat16 [1024, 32], P(None, 'head'), may hold values from -0.1875 to 0.1875
- conv_x_weight: float32 [2048, 4], P('head'), may hold values from -3 to 3
- conv_x_bias: float32 [2048], P('head'), may hold values from -0.5 to 0.5
- conv_bc_weight: float32 [256, 4], P('head'), may hold values from -3 to 3
- conv_bc_bias: float32 [256], P('head'), may hold values from -0.5 to 0.5
- dt_bias: float32 [32], P('head'), may hold values from -1 to 1
- decay_rate: float32 [32], P('head'), may hold values from 1e-05 to 0.3
- skip: float32 [32], P('head'), may hold values from 0.5 to 1.5
- gate_gain: float32 [2048], P('head'), may hold values from 0.5 to 1.5
- w_out: bfloat16 [2048, 1024], P('head'), may hold values from -0.125 to 0.125
- cotangent: bfloat16 [4096, 1024], P('seq'), may hold values from -6 to 6
Outputs:
- block_output: bfloat16 [4096, 1024], P('seq', 'head')
- input_grad: float32 [4096, 1024], P('seq', 'head')
- norm_gain_grad: float32 [1024], P('head')
- w_zx_grad: float32 [1024, 2, 2048], P('seq', None, 'head')
- w_bc_grad: float32 [1024, 256], P('seq', 'head')
- w_dt_grad: float32 [1024, 32], P('seq', 'head')
- conv_x_weight_grad: float32 [2048, 4], P('head')
- conv_x_bias_grad: float32 [2048], P('head')
- conv_bc_weight_grad: float32 [256, 4], P('head')
- conv_bc_bias_grad: float32 [256], P('head')
- dt_bias_grad: float32 [32], P('head')
- decay_rate_grad: float32 [32], P('head')
- skip_grad: float32 [32], P('head')
- gate_gain_grad: float32 [2048], P('head')
- w_out_grad: float32 [2048, 1024], P('head', 'seq')
The draws below stay inside these ranges and needn't reach their ends.
Inputs may be any that keep to these rules, and one draw needn't show every extreme that they name: `seq_pieces`: the lengths add up to 16; the third sequence is the longest, exactly 4, and covers pieces 16 // 2 - 2 to 9.
All inputs are finite; a program needn't handle non-finite values.
Results may differ from the reference program's by a relative error of at most 0.0019.
The reference program's roundings to bfloat16 on the way (of `normed_bf`, `mixed` and `d_zx`) count: a program that leaves them out, or rounds other values in their place, can miss the bound.
Values sent between devices are 32-bit elements; how exact they have to be, the bound alone decides.
A program may use at most 192 MiB of HBM per device.

```python
import math
import jax
import jax.numpy as jnp
from jax import lax

D = 1024
H = 32
P_SIZE = 64
N = 128
DI = 2048
K = 4
SPAN = 256
TOK_DEV = 256
PIECES = 16
MOST = 4
TOKENS = 4096


def draw_decay_rate(key, part):
    key_pick, key_slow, key_fast = jax.random.split(key, 3)
    slow_share = 0.5
    pick_values = jax.random.uniform(key_pick, (H,), jnp.float32)
    slow_rates = jnp.exp(jax.random.uniform(key_slow, (H,), jnp.float32, math.log(1e-05), math.log(0.0001)))
    fast_rates = jnp.exp(jax.random.uniform(key_fast, (H,), jnp.float32, math.log(0.03), math.log(0.3)))
    return jnp.where(pick_values < slow_share, slow_rates, fast_rates).astype(jnp.float32)


def draw_seq_pieces(key, part):
    key_offset, key_left, key_right = jax.random.split(jax.random.fold_in(key, 7103), 3)
    middle = PIECES // 2
    offset = jax.random.randint(key_offset, (), 2, MOST - 1)
    left_total = middle - offset
    right_total = PIECES - left_total - MOST
    first_len = jax.random.randint(key_left, (), jnp.maximum(1, left_total - MOST), jnp.minimum(MOST, left_total - 1) + 1)
    fourth_len = jax.random.randint(key_right, (), jnp.maximum(1, right_total - MOST), jnp.minimum(MOST, right_total - 1) + 1)
    longest = jnp.full((), MOST, jnp.int32)
    return jnp.stack([first_len, left_total - first_len, longest, fourth_len, right_total - fourth_len]).astype(jnp.int32)


def raised(entries, rng, source, target, parts, factor):
    owner, partner = [(jnp.arange(entries.shape[axis_at]) // (entries.shape[axis_at] // parts)).reshape([-1 if axis == axis_at else 1 for axis in range(entries.ndim)]) for axis_at in (source, target)]
    chosen = jax.random.permutation(rng, parts)[partner]
    strong = (owner == chosen) | (owner == (partner + parts // 2) % parts)
    return jnp.where(strong, factor * entries, entries)


def block_scale(stream_key, dims, cuts, smallest, largest):
    factor_of = 1.0
    for dim, blocks in cuts:
        heights = jax.random.uniform(jax.random.fold_in(jax.random.fold_in(stream_key, 6), dim), (blocks,), jnp.float32, smallest / len(cuts), largest / len(cuts))
        factor_of = factor_of * jnp.repeat(jnp.exp(heights), dims[dim] // blocks).reshape((-1,) + (1,) * (len(dims) - 1 - dim))
    return factor_of


def bell_draw(key, dims, scale, limit, shards=(), held_as=jnp.bfloat16):
    values = scale * jax.random.normal(key, dims, jnp.float32)
    if shards:
        values = values * block_scale(key, dims, shards, -0.22, 0.18)
    return jnp.clip(values, -limit, limit).astype(held_as)


def bell_draw_with(stream_key, shape, width, most, shards, heavy, kind=jnp.bfloat16):
    values = width * jax.random.normal(stream_key, shape, jnp.float32)
    if shards:
        values = values * block_scale(stream_key, shape, shards, -0.22, 0.18)
    return jnp.clip(raised(values, jax.random.fold_in(stream_key, 3), *heavy), -most, most).astype(kind)


def setup_inputs(seed: int = 0) -> dict:
    splits = jax.random.split(jax.random.key(seed), 17)
    return {
        "block_input": bell_draw_with(splits[0], (TOKENS, D), 1.0, 6.0, ((0, 16),), (0, 1, 16, 2.0)),
        "seq_pieces": draw_seq_pieces(jax.random.fold_in(splits[16], 71), 0),
        "norm_gain": jnp.clip(1.0 + 0.1 * jax.random.normal(splits[2], (D,), jnp.float32), 0.5, 1.5),
        "w_zx": bell_draw(splits[3], (D, 2, DI), D ** -0.5, 0.1875, ((2, 2),)),
        "w_bc": bell_draw(splits[4], (D, 2 * N), D ** -0.5, 0.1875, ((1, 2),)),
        "w_dt": bell_draw(splits[5], (D, H), D ** -0.5, 0.1875, ((1, 2),)),
        "conv_x_weight": bell_draw(splits[6], (DI, K), K ** -0.5, 3.0, ((0, 2),), jnp.float32),
        "conv_x_bias": jnp.clip(jax.random.uniform(splits[7], (DI,), jnp.float32, -0.5, 0.5) * block_scale(splits[7], (DI,), ((0, 2),), -0.4, 0.0), -0.5, 0.5),
        "conv_bc_weight": bell_draw(splits[8], (2 * N, K), K ** -0.5, 3.0, ((0, 2),), jnp.float32),
        "conv_bc_bias": jnp.clip(jax.random.uniform(splits[9], (2 * N,), jnp.float32, -0.5, 0.5) * block_scale(splits[9], (2 * N,), ((0, 2),), -0.4, 0.0), -0.5, 0.5),
        "dt_bias": jnp.clip(jax.random.uniform(splits[10], (H,), jnp.float32, -1.0, 1.0) * block_scale(splits[10], (H,), ((0, 2),), -0.4, 0.0), -1.0, 1.0),
        "decay_rate": draw_decay_rate(jax.random.fold_in(splits[16], 71), 0),
        "skip": jnp.clip(0.5 + 1.0 * jax.random.uniform(splits[12], (H,), jnp.float32) ** block_scale(splits[12], (H,), ((0, 2),), -0.2, 0.2), 0.5, 1.5),
        "gate_gain": jnp.clip(1.0 + 0.1 * jax.random.normal(splits[13], (DI,), jnp.float32), 0.5, 1.5),
        "w_out": bell_draw(splits[14], (DI, D), DI ** -0.5, 0.125, ((0, 2),)),
        "cotangent": bell_draw_with(splits[15], (TOKENS, D), 1.0, 6.0, ((0, 16),), (0, 1, 16, 2.0)),
    }


EPS = 1e-05

def silu(values):
    return values * jax.nn.sigmoid(values)

def input_norm(values, gain):
    scale = lax.rsqrt(lax.optimization_barrier(jnp.mean(values * values, axis=-1, keepdims=True)) + EPS)
    return values * scale * gain

def conv_act(conv_pre, edge_prev, weight, bias):
    width_taps = weight.shape[1]
    total_rows = conv_pre.shape[0]
    extended = jnp.concatenate([edge_prev, conv_pre], axis=0)
    result = bias[None, :] + extended[0:total_rows] * weight[:, 0][None, :]
    for lag_index in range(1, width_taps):
        result = result + extended[lag_index:lag_index + total_rows] * weight[:, lag_index][None, :]
    return silu(result)

def ssd_local(x_act, b_mat, c_mat, dt_raw, dt_shift, rates, block):
    total_rows, head_num, head_size = x_act.shape
    block_count = total_rows // block
    highest = lax.Precision.HIGHEST
    step_size = jax.nn.softplus(dt_raw + dt_shift[None, :]).T
    cumul = jnp.cumsum(-step_size * rates[:, None], axis=1)
    causal = (jnp.arange(block)[:, None] >= jnp.arange(block)[None, :])[None, :, :]
    x_heads = jnp.transpose(x_act, (1, 0, 2))

    def one_block(carry, inputs_block):
        state_now, level_before = carry
        x_block, b_block, c_block, step_block, cumul_block = inputs_block
        scores = jnp.dot(c_block, b_block.T, precision=highest)
        spread = jnp.where(causal, cumul_block[:, :, None] - cumul_block[:, None, :], -jnp.inf)
        weights = scores[None, :, :] * jnp.exp(spread) * step_block[:, None, :]
        inside = jnp.einsum('hts,hsp->htp', weights, x_block, precision=highest)
        carried = jnp.exp(cumul_block - level_before[:, None])[:, :, None] * jnp.einsum('tn,hpn->htp', c_block, state_now, precision=highest)
        level_after = cumul_block[:, -1]
        tail_weight = jnp.exp(level_after[:, None] - cumul_block) * step_block
        fresh_state = jnp.einsum('hsp,sn->hpn', tail_weight[:, :, None] * x_block, b_block, precision=highest)
        state_next = jnp.exp(level_after - level_before)[:, None, None] * state_now + fresh_state
        return ((state_next, level_after), inside + carried)

    def rows_blocks(values):
        return values.reshape((block_count, block) + values.shape[1:])

    def head_blocks(values):
        shaped = values.reshape((values.shape[0], block_count, block) + values.shape[2:])
        return jnp.moveaxis(shaped, 1, 0)
    initial = (jnp.zeros((head_num, head_size, b_mat.shape[1]), jnp.float32), jnp.zeros((head_num,), jnp.float32))
    (state_end, level_end), outputs = lax.scan(one_block, initial, (head_blocks(x_heads), rows_blocks(b_mat), rows_blocks(c_mat), head_blocks(step_size), head_blocks(cumul)))
    outputs = jnp.transpose(outputs, (0, 2, 1, 3)).reshape(total_rows, head_num, head_size)
    return (outputs, state_end, jnp.exp(level_end), cumul.T)

def inter_term(c_mat, cumul, state_in):
    return jnp.exp(cumul)[:, :, None] * jnp.einsum('tn,hpn->thp', c_mat, state_in, precision=lax.Precision.HIGHEST)

def reference(block_input, seq_pieces, norm_gain, w_zx, w_bc, w_dt, conv_x_weight, conv_x_bias, conv_bc_weight, conv_bc_bias, dt_bias, decay_rate, skip, gate_gain, w_out, cotangent):
    inner_all = H * P_SIZE
    edge_rows = K - 1
    zx_flat = w_zx.reshape(D, 2 * inner_all)
    x_weight = w_zx[:, 1, :]
    conv_weight = jnp.concatenate([conv_x_weight, conv_bc_weight], axis=0)
    conv_bias = jnp.concatenate([conv_x_bias, conv_bc_bias], axis=0)
    bounds = jnp.cumsum(seq_pieces).astype(jnp.int32)
    first_pieces = jnp.concatenate([jnp.zeros((1,), jnp.int32), bounds[:-1].astype(jnp.int32)])
    piece_ids = jnp.arange(PIECES, dtype=jnp.int32)
    keep_all = 1.0 - jnp.any(piece_ids[:, None] == first_pieces[None, :], axis=1).astype(jnp.float32)
    input_blocks = block_input.reshape(PIECES, TOK_DEV, D)
    cot_blocks = cotangent.reshape(PIECES, TOK_DEV, D)

    def split_act(activated):
        x_act = activated[:, :inner_all].reshape(TOK_DEV, H, P_SIZE)
        return (x_act, activated[:, inner_all:inner_all + N], activated[:, inner_all + N:])

    def local_scan(x_act, b_mat, c_mat, dt_raw, dt_shift, rates):
        return ssd_local(x_act, b_mat, c_mat, dt_raw, dt_shift, rates, SPAN)

    def forward_step(carry, scanned):
        state_end, edge_last = carry
        block_rows, keep_piece = scanned
        normed_bf = input_norm(block_rows.astype(jnp.float32), norm_gain).astype(jnp.bfloat16)
        x_pre = jnp.dot(normed_bf, x_weight, preferred_element_type=jnp.float32)
        bc_pre = jnp.dot(normed_bf, w_bc, preferred_element_type=jnp.float32)
        dt_raw = jnp.dot(normed_bf, w_dt, preferred_element_type=jnp.float32)
        conv_pre = jnp.concatenate([x_pre, bc_pre], axis=1)
        edge_prev = edge_last * keep_piece
        x_act, b_mat, c_mat = split_act(conv_act(conv_pre, edge_prev, conv_weight, conv_bias))
        y_local, piece_state, piece_decay, cumul = local_scan(x_act, b_mat, c_mat, dt_raw, dt_bias, decay_rate)
        state_in = state_end * keep_piece
        state_next = piece_decay[:, None, None] * state_in + piece_state
        return ((state_next, conv_pre[TOK_DEV - edge_rows:]), (state_in, edge_prev))
    start_carry = (jnp.zeros((H, P_SIZE, N), jnp.float32), jnp.zeros((edge_rows, inner_all + 2 * N), jnp.float32))
    unused_carry, (states_in, edges_prev) = lax.scan(forward_step, start_carry, (input_blocks, keep_all))

    def backward_step(carry, scanned):
        grad_end, tail_grad, sums = carry
        block_rows, cot_rows, keep_piece, state_in, edge_prev = scanned
        inputs32 = block_rows.astype(jnp.float32)
        normed, norm_pullback = jax.vjp(input_norm, inputs32, norm_gain)
        normed_bf = normed.astype(jnp.bfloat16)
        zx_proj = jnp.dot(normed_bf, zx_flat, preferred_element_type=jnp.float32).reshape(TOK_DEV, 2, inner_all)
        bc_pre = jnp.dot(normed_bf, w_bc, preferred_element_type=jnp.float32)
        dt_raw = jnp.dot(normed_bf, w_dt, preferred_element_type=jnp.float32)
        gate_pre = zx_proj[:, 0]
        conv_pre = jnp.concatenate([zx_proj[:, 1], bc_pre], axis=1)
        activated, conv_pullback = jax.vjp(conv_act, conv_pre, edge_prev, conv_weight, conv_bias)
        x_act, b_mat, c_mat = split_act(activated)
        (y_local, piece_state, piece_decay, cumul), ssd_pullback = jax.vjp(local_scan, x_act, b_mat, c_mat, dt_raw, dt_bias, decay_rate)
        carried, inter_pullback = jax.vjp(inter_term, c_mat, cumul, state_in)
        y_ssm = y_local + carried + skip[None, :, None] * x_act
        y_flat = y_ssm.reshape(TOK_DEV, inner_all)
        z_silu = silu(gate_pre)
        gated = y_flat * z_silu
        gate_scale = lax.rsqrt(lax.optimization_barrier(jnp.mean(gated * gated, axis=1, keepdims=True)) + EPS)
        gate_hat = gated * gate_scale
        mixed = (gate_hat * gate_gain[None, :]).astype(jnp.bfloat16)
        out_rows = (inputs32 + jnp.dot(mixed, w_out, preferred_element_type=jnp.float32)).astype(jnp.bfloat16)
        d_mixed = jnp.dot(cot_rows, w_out.T, preferred_element_type=jnp.float32)
        w_out_term = jnp.dot(mixed.T, cot_rows, preferred_element_type=jnp.float32)
        gate_gain_term = lax.optimization_barrier(jnp.sum(d_mixed * gate_hat, axis=0))
        d_hat = d_mixed * gate_gain[None, :]
        row_mean = lax.optimization_barrier(jnp.mean(d_hat * gate_hat, axis=1, keepdims=True))
        d_gated = gate_scale * (d_hat - gate_hat * row_mean)
        sigma = jax.nn.sigmoid(gate_pre)
        d_yssm = (d_gated * z_silu).reshape(TOK_DEV, H, P_SIZE)
        d_gate_pre = d_gated * y_flat * sigma * (1.0 + gate_pre * (1.0 - sigma))
        skip_term = lax.optimization_barrier(jnp.sum(d_yssm * x_act, axis=(0, 2)))
        d_cinter, d_cumul, d_state_local = inter_pullback(d_yssm)
        d_decay = lax.optimization_barrier(jnp.sum(grad_end * state_in, axis=(1, 2)))
        d_x, d_b, d_c, d_raw, dt_bias_term, rate_term = ssd_pullback((d_yssm, grad_end, d_decay, d_cumul))
        grad_start = keep_piece * (d_state_local + piece_decay[:, None, None] * grad_end)
        d_x = d_x + skip[None, :, None] * d_yssm
        d_act = jnp.concatenate([d_x.reshape(TOK_DEV, inner_all), d_b, d_c + d_cinter], axis=1)
        d_conv_pre, d_edge, conv_w_term, conv_b_term = conv_pullback(d_act)
        d_conv_pre = jnp.concatenate([d_conv_pre[:TOK_DEV - edge_rows], d_conv_pre[TOK_DEV - edge_rows:] + tail_grad], axis=0)
        d_zx = jnp.stack([d_gate_pre, d_conv_pre[:, :inner_all]], axis=1).reshape(TOK_DEV, 2 * inner_all).astype(jnp.bfloat16)
        d_bc = d_conv_pre[:, inner_all:].astype(jnp.bfloat16)
        d_dt = d_raw.astype(jnp.bfloat16)
        d_normed = jnp.dot(d_zx, zx_flat.T, preferred_element_type=jnp.float32)
        d_normed = d_normed + jnp.dot(d_bc, w_bc.T, preferred_element_type=jnp.float32)
        d_normed = d_normed + jnp.dot(d_dt, w_dt.T, preferred_element_type=jnp.float32)
        d_inputs, gain_term = norm_pullback(d_normed)
        grad_rows = cot_rows.astype(jnp.float32) + d_inputs
        terms = (gain_term, jnp.dot(normed_bf.T, d_zx, preferred_element_type=jnp.float32), jnp.dot(normed_bf.T, d_bc, preferred_element_type=jnp.float32), jnp.dot(normed_bf.T, d_dt, preferred_element_type=jnp.float32), conv_w_term, conv_b_term, dt_bias_term, rate_term, skip_term, gate_gain_term, w_out_term)
        sums = jax.tree.map(jnp.add, sums, terms)
        return ((grad_start, d_edge * keep_piece, sums), (out_rows, grad_rows))
    zero_sums = (jnp.zeros((D,), jnp.float32), jnp.zeros((D, 2 * inner_all), jnp.float32), jnp.zeros((D, 2 * N), jnp.float32), jnp.zeros((D, H), jnp.float32), jnp.zeros((inner_all + 2 * N, K), jnp.float32), jnp.zeros((inner_all + 2 * N,), jnp.float32), jnp.zeros((H,), jnp.float32), jnp.zeros((H,), jnp.float32), jnp.zeros((H,), jnp.float32), jnp.zeros((inner_all,), jnp.float32), jnp.zeros((inner_all, D), jnp.float32))
    back_carry = (jnp.zeros((H, P_SIZE, N), jnp.float32), jnp.zeros((edge_rows, inner_all + 2 * N), jnp.float32), zero_sums)
    final_carry, (out_blocks, grad_blocks) = lax.scan(backward_step, back_carry, (input_blocks, cot_blocks, keep_all, states_in, edges_prev), reverse=True)
    sums = final_carry[2]
    block_output = out_blocks.reshape(TOKENS, D)
    input_grad = grad_blocks.reshape(TOKENS, D)
    conv_w_all = sums[4]
    conv_b_all = sums[5]
    return (block_output, input_grad, sums[0], sums[1].reshape(D, 2, inner_all), sums[2], sums[3], conv_w_all[:inner_all], conv_b_all[:inner_all], conv_w_all[inner_all:], conv_b_all[inner_all:], sums[6], sums[7], sums[8], sums[9], sums[10])
```

```python
import jax
import jax.numpy as jnp
from jax import lax
from jax.sharding import PartitionSpec as P

EPS = 1e-05
HIGH = lax.Precision.HIGH
F32 = jnp.float32
BF16 = jnp.bfloat16


def shifted(value, steps):
    count = lax.axis_size("seq")
    initial, last = (max(0, -steps), min(count, count - steps))
    return lax.ppermute(value, "seq", [(s, s + steps) for s in range(initial, last)])


def other_core(value):
    return lax.ppermute(value, "head", [(0, 1), (1, 0)])


def bit_orders(count):
    bits = count.bit_length() - 1
    first = list(range(bits))
    second = list(first)
    if bits > 1:
        second[0], second[1] = (second[1], second[0])
    return (first, second)


def swap(value, phase):
    count = lax.axis_size("seq")
    orders = bit_orders(count)
    pairs = [
        (s * 2 + core, (s ^ (1 << orders[core][phase])) * 2 + core)
        for s in range(count)
        for core in range(2)
    ]
    return lax.ppermute(value, ("seq", "head"), pairs)


def own_first(matrix):
    count = lax.axis_size("seq")
    bits = count.bit_length() - 1
    rows = matrix.shape[0] // count
    core = lax.axis_index("head")
    place = lax.axis_index("seq")
    blocks = []
    for k in range(count):
        masks = [
            sum(((k >> (bits - 1 - i)) & 1) << order[i] for i in range(bits))
            for order in bit_orders(count)
        ]
        source = place ^ jnp.where(core == 0, masks[0], masks[1])
        blocks.append(lax.dynamic_slice_in_dim(matrix, source * rows, rows, 0))
    return jnp.concatenate(blocks, axis=0)


def mm(a, b):
    return jnp.dot(a, b, preferred_element_type=F32)


def scatter_sum(left, right):
    count = lax.axis_size("seq")
    half = left.shape[0] // 2
    total = swap(mm(left[half:], right), 0) + mm(left[:half], right)
    for phase in range(1, count.bit_length() - 1):
        half = half // 2
        total = total[:half] + swap(total[half:], phase)
    return total


def total_sum(value):
    for phase in range(lax.axis_size("seq").bit_length() - 1):
        value = value + swap(value, phase)
    return value


def compose_from(decay, state, hops, sign):
    if hops <= 3:
        decays = [shifted(decay, sign * k) for k in range(1, hops)]
        states = [shifted(state, sign * k) for k in range(1, hops + 1)]
        result = states[-1]
        for k in range(hops - 2, -1, -1):
            result = states[k] + decays[k][:, None, None] * result
        return result
    decay, state = (shifted(decay, sign), shifted(state, sign))
    reach = 1
    while reach < hops:
        far_decay, far_state = (shifted(decay, sign * reach), shifted(state, sign * reach))
        state = state + decay[:, None, None] * far_state
        decay = decay * far_decay
        reach *= 2
    return state


def silu(values):
    return values * jax.nn.sigmoid(values)


def conv_act(conv_pre, edge_prev, weight, bias):
    width_taps = weight.shape[1]
    total_rows = conv_pre.shape[0]
    extended = jnp.concatenate([edge_prev, conv_pre], axis=0)
    result = bias[None, :] + extended[0:total_rows] * weight[:, 0][None, :]
    for lag_index in range(1, width_taps):
        result = (
            result + extended[lag_index : lag_index + total_rows] * weight[:, lag_index][None, :]
        )
    return silu(result)


def on_device(
    block_input,
    seq_pieces,
    norm_gain,
    w_zx,
    w_bc,
    w_dt,
    conv_x_weight,
    conv_x_bias,
    conv_bc_weight,
    conv_bc_bias,
    dt_bias,
    decay_rate,
    skip,
    gate_gain,
    w_out,
    cotangent,
):
    tok_rows, model_width = block_input.shape
    inner_own = w_zx.shape[2]
    heads_own = w_dt.shape[1]
    head_size = inner_own // heads_own
    edge_rows = conv_x_weight.shape[1] - 1
    inner_all = inner_own * lax.axis_size("head")
    width_own = model_width // lax.axis_size("head")
    hops = max(1, lax.axis_size("seq") // 4 - 1)
    first_core = lax.axis_index("head") == 0
    piece_index = lax.axis_index("seq")
    bounds = jnp.cumsum(seq_pieces)
    first_pieces = jnp.concatenate([jnp.zeros((1,), jnp.int32), bounds[:-1]])
    keep_own = 1.0 - jnp.any(first_pieces == piece_index).astype(F32)

    def own_half(values):
        return jnp.where(first_core, values[:, :width_own], values[:, width_own:])

    def far_half(values):
        return jnp.where(first_core, values[:, width_own:], values[:, :width_own])

    inputs32 = block_input.astype(F32)
    in_scale = lax.rsqrt(jnp.mean(inputs32 * inputs32, axis=-1, keepdims=True) + EPS)
    normed_bf = (inputs32 * in_scale * norm_gain).astype(BF16)
    w_z = w_zx[:, 0]
    w_x = w_zx[:, 1]
    dt_raw = mm(normed_bf, w_dt)
    bc_pre = mm(normed_bf, w_bc)
    x_pre = mm(normed_bf, w_x)
    conv_pre = jnp.concatenate([x_pre, bc_pre], axis=1)
    conv_weight = jnp.concatenate([conv_x_weight, conv_bc_weight], axis=0)
    conv_bias = jnp.concatenate([conv_x_bias, conv_bc_bias], axis=0)
    edge_prev = shifted(conv_pre[tok_rows - edge_rows :], 1) * keep_own
    activated, conv_pullback = jax.vjp(conv_act, conv_pre, edge_prev, conv_weight, conv_bias)
    gate_pre = mm(normed_bf, w_z)
    x_flat = activated[:, :inner_own]
    bc_own = activated[:, inner_own:]
    bc_far = other_core(bc_own)
    b_mat = jnp.where(first_core, bc_own, bc_far)
    c_mat = jnp.where(first_core, bc_far, bc_own)

    shifted_raw = (dt_raw + dt_bias[None, :]).T
    step = jax.nn.softplus(shifted_raw)
    cumul = jnp.cumsum(-step * decay_rate[:, None], axis=1)
    level = cumul[:, -1]
    decay = jnp.exp(level)
    x_act = jnp.transpose(x_flat.reshape(tok_rows, heads_own, head_size), (1, 0, 2))
    x_step = x_act * step[:, :, None]
    tail = jnp.exp(level[:, None] - cumul)
    piece_state = jnp.einsum("hsp,sn->hpn", tail[:, :, None] * x_step, b_mat, precision=HIGH)
    prefix = compose_from(decay * keep_own, piece_state, hops, 1)
    state_in = prefix * keep_own
    causal = (jnp.arange(tok_rows)[:, None] >= jnp.arange(tok_rows)[None, :])[None, :, :]
    scores = jnp.dot(c_mat, b_mat.T, precision=HIGH)
    spread = jnp.exp(jnp.where(causal, cumul[:, :, None] - cumul[:, None, :], -jnp.inf))
    weights = scores[None] * spread
    y_inside = jnp.einsum("hts,hsp->htp", weights, x_step, precision=HIGH)
    grown = jnp.exp(cumul)
    y_scan = y_inside + grown[:, :, None] * jnp.einsum(
        "tn,hpn->htp", c_mat, state_in, precision=HIGH
    )

    def flat(values):
        return jnp.transpose(values, (1, 0, 2)).reshape(tok_rows, inner_own)

    y_flat = flat(y_scan + skip[:, None, None] * x_act)
    d_mixed = mm(cotangent, w_out.T)
    sigma = jax.nn.sigmoid(gate_pre)
    z_silu = gate_pre * sigma
    gated = y_flat * z_silu
    d_hat = d_mixed * gate_gain[None, :]
    row_sums = jnp.stack([jnp.sum(gated * gated, axis=1), jnp.sum(d_hat * gated, axis=1)])
    row_sums = row_sums + other_core(row_sums)
    gate_scale = lax.rsqrt(row_sums[0] / inner_all + EPS)[:, None]
    gate_hat = gated * gate_scale
    row_dots = row_sums[1][:, None] * gate_scale
    mixed = (gate_hat * gate_gain[None, :]).astype(BF16)
    d_gated = gate_scale * (d_hat - gate_hat * (row_dots / inner_all))
    d_y_flat = d_gated * z_silu
    d_gate = (d_gated * y_flat * sigma * (1.0 + gate_pre * (1.0 - sigma))).astype(BF16)
    gate_gain_term = jnp.sum(d_mixed * gate_hat, axis=0)
    d_y = jnp.transpose(d_y_flat.reshape(tok_rows, heads_own, head_size), (1, 0, 2))

    d_y_grown = d_y * grown[:, :, None]
    d_state_local = jnp.einsum("htp,tn->hpn", d_y_grown, c_mat, precision=HIGH)
    grad_end = compose_from(decay * keep_own, d_state_local * keep_own, hops, -1)

    cot_rows = own_first(cotangent.T)
    normed_rows = own_first(normed_bf.T)
    out_grad = scatter_sum(cot_rows, mixed).T
    z_grad = scatter_sum(normed_rows, d_gate)

    out_terms = mm(mixed, w_out)
    block_output = (
        own_half(inputs32) + (own_half(out_terms) + other_core(far_half(out_terms)))
    ).astype(BF16)

    skip_term = jnp.sum(d_y * x_act, axis=(1, 2))
    d_inside = jnp.einsum("hts,htp->hsp", weights, d_y, precision=HIGH)
    d_scores = jnp.sum(
        jnp.einsum("htp,hsp->hts", d_y, x_step, precision=HIGH) * spread, axis=0
    )
    d_c = jnp.dot(d_scores, b_mat, precision=HIGH) + jnp.einsum(
        "htp,hpn->tn", d_y_grown, state_in, precision=HIGH
    )
    d_b = jnp.dot(d_scores.T, c_mat, precision=HIGH)
    d_b = d_b + jnp.einsum("hsp,hpn->sn", tail[:, :, None] * x_step, grad_end, precision=HIGH)
    d_x_step = d_inside + tail[:, :, None] * jnp.einsum(
        "hpn,sn->hsp", grad_end, b_mat, precision=HIGH
    )
    d_step = jnp.sum(x_act * d_x_step, axis=2)
    d_cumul = jnp.sum(d_y * y_scan, axis=2) - step * d_step
    d_level = jnp.sum(grad_end * (decay[:, None, None] * state_in + piece_state), axis=(1, 2))
    d_cumul = d_cumul.at[:, -1].add(d_level)
    d_log = jnp.cumsum(d_cumul[:, ::-1], axis=1)[:, ::-1]
    rate_term = -jnp.sum(step * d_log, axis=1)
    d_raw = (d_step - decay_rate[:, None] * d_log) * jax.nn.sigmoid(shifted_raw)
    dt_bias_term = jnp.sum(d_raw, axis=1)
    d_x = flat(step[:, :, None] * d_x_step + skip[:, None, None] * d_y)

    bc_own_grad = jnp.where(first_core, d_b, d_c) + other_core(jnp.where(first_core, d_c, d_b))
    d_act = jnp.concatenate([d_x, bc_own_grad], axis=1)
    d_conv_pre, d_edge, conv_w_term, conv_b_term = conv_pullback(d_act)
    tail_grad = shifted(d_edge * keep_own, -1)
    d_conv_pre = jnp.concatenate(
        [d_conv_pre[: tok_rows - edge_rows], d_conv_pre[tok_rows - edge_rows :] + tail_grad], axis=0
    )
    d_x_pre = d_conv_pre[:, :inner_own].astype(BF16)
    d_bc = d_conv_pre[:, inner_own:].astype(BF16)
    d_dt = d_raw.T.astype(BF16)
    padded = jnp.pad(d_dt, ((0, 0), (0, -heads_own % 128)))
    x_grad = scatter_sum(normed_rows, jnp.concatenate([d_x_pre, d_bc, padded], axis=1))
    state_own = w_bc.shape[1]

    norm_terms = mm(d_gate, w_z.T)
    norm_terms = norm_terms + mm(d_x_pre, w_x.T)
    norm_terms = norm_terms + mm(d_bc, w_bc.T)
    norm_terms = norm_terms + mm(d_dt, w_dt.T)
    in_hat = inputs32 * in_scale
    row_dot = jnp.sum(norm_terms * norm_gain * in_hat, axis=1)
    row_dot = row_dot + other_core(row_dot)
    d_normed_own = own_half(norm_terms) + other_core(far_half(norm_terms))
    own_gain = jnp.where(first_core, norm_gain[:width_own], norm_gain[width_own:])
    own_hat = own_half(in_hat)
    input_grad = (
        in_scale * (d_normed_own * own_gain - own_hat * (row_dot[:, None] / model_width))
        + own_half(cotangent).astype(F32)
    )
    gain_own = jnp.sum(d_normed_own * own_hat, axis=0)

    terms = (
        gain_own,
        gate_gain_term,
        conv_w_term.T.reshape(-1),
        conv_b_term,
        dt_bias_term,
        rate_term,
        skip_term,
    )
    packed = total_sum(jnp.concatenate(terms))
    sums = []
    offset = 0
    for term in terms:
        sums.append(packed[offset : offset + term.shape[0]])
        offset += term.shape[0]
    conv_w = sums[2].reshape(edge_rows + 1, -1).T
    zx_grad = jnp.stack([z_grad, x_grad[:, :inner_own]], axis=1)
    return (
        block_output,
        input_grad,
        sums[0],
        zx_grad,
        x_grad[:, inner_own : inner_own + state_own],
        x_grad[:, inner_own + state_own : inner_own + state_own + heads_own],
        conv_w[:inner_own],
        sums[3][:inner_own],
        conv_w[inner_own:],
        sums[3][inner_own:],
        sums[4],
        sums[5],
        sums[6],
        sums[1],
        out_grad,
    )


def solution(mesh):
    placed = (
        P("seq", None),
        P(),
        P(),
        P(None, None, "head"),
        P(None, "head"),
        P(None, "head"),
        P("head", None),
        P("head"),
        P("head", None),
        P("head"),
        P("head"),
        P("head"),
        P("head"),
        P("head"),
        P("head", None),
        P("seq", None),
    )
    return jax.shard_map(
        on_device,
        mesh=mesh,
        in_specs=placed,
        out_specs=(
            P("seq", "head"),
            P("seq", "head"),
            P("head"),
            P("seq", None, "head"),
            P("seq", "head"),
            P("seq", "head"),
            P("head", None),
            P("head"),
            P("head", None),
            P("head"),
            P("head"),
            P("head"),
            P("head"),
            P("head"),
            P("head", "seq"),
        ),
        check_vma=False,
    )
```

```python
import jax
import jax.numpy as jnp
from jax import lax
from jax.sharding import PartitionSpec as P


EPS = 1e-05
HIGH = lax.Precision.HIGH
F32 = jnp.float32
BF16 = jnp.bfloat16


def shifted(value, steps):
    count = lax.axis_size("seq")
    initial, last = (max(0, -steps), min(count, count - steps))
    return lax.ppermute(value, "seq", [(s, s + steps) for s in range(initial, last)])


def other_core(value):
    return lax.ppermute(value, "head", [(0, 1), (1, 0)])


def bit_orders(count, late):
    bits = count.bit_length() - 1
    low = list(range(min(2, bits)))
    high = list(range(len(low), bits))
    if late:
        return (high + low, high + low[::-1])
    return (low + high, low[::-1] + high)


def swap(value, phase, late):
    count = lax.axis_size("seq")
    orders = bit_orders(count, late)
    pairs = [
        (s * 2 + core, (s ^ (1 << orders[core][phase])) * 2 + core)
        for s in range(count)
        for core in range(2)
    ]
    return lax.ppermute(value, ("seq", "head"), pairs)


def own_first(matrix, late):
    count = lax.axis_size("seq")
    bits = count.bit_length() - 1
    width = matrix.shape[1]
    each = width // count
    masks = [
        [sum(((k >> (bits - 1 - i)) & 1) << order[i] for i in range(bits)) for k in range(count)]
        for order in bit_orders(count, late)
    ]
    mask = jnp.where(
        lax.axis_index("head") == 0,
        jnp.asarray(masks[0], jnp.int32),
        jnp.asarray(masks[1], jnp.int32),
    )
    source = (lax.axis_index("seq") ^ mask)[:, None] * each + jnp.arange(each)[None, :]
    chosen = (jnp.arange(width)[:, None] == source.reshape(1, width)).astype(BF16)
    return mm(matrix, chosen).astype(BF16)


def mm(a, b):
    return jnp.dot(a, b, preferred_element_type=F32)


def mm_rows(a, b):
    return lax.dot_general(a, b, (((0,), (0,)), ((), ())), preferred_element_type=F32)


def scatter_sum(left, right, late):
    count = lax.axis_size("seq")
    half = left.shape[1] // 2
    total = swap(mm_rows(left[:, half:], right), 0, late) + mm_rows(left[:, :half], right)
    for phase in range(1, count.bit_length() - 1):
        half = half // 2
        total = total[:half] + swap(total[half:], phase, late)
    return total


def total_sum(value):
    for phase in range(lax.axis_size("seq").bit_length() - 1):
        value = value + swap(value, phase, False)
    return value


def compose_from(decay, state, hops, sign):
    if hops <= 3:
        heads = decay.shape[0]
        row = jnp.zeros((1,) + state.shape[1:], F32)
        row = row + jnp.pad(decay, (0, state.shape[2] - heads))[None, None, :]
        packed = jnp.concatenate([state, row], axis=0)
        parts = []
        for k in range(1, hops + 1):
            parts.append(shifted(packed, sign * k))
        result = parts[-1][:heads]
        for part in parts[-2::-1]:
            result = part[:heads] + part[heads, 0, :heads][:, None, None] * result
        return result
    decay, state = (shifted(decay, sign), shifted(state, sign))
    reach = 1
    while reach < hops:
        far_decay, far_state = (shifted(decay, sign * reach), shifted(state, sign * reach))
        state = state + decay[:, None, None] * far_state
        decay = decay * far_decay
        reach *= 2
    return state


def silu(values):
    return values * jax.nn.sigmoid(values)


def conv_act(conv_pre, edge_prev, weight, bias):
    width_taps = weight.shape[1]
    total_rows = conv_pre.shape[0]
    extended = jnp.concatenate([edge_prev, conv_pre], axis=0)
    result = bias[None, :] + extended[0:total_rows] * weight[:, 0][None, :]
    for lag_index in range(1, width_taps):
        result = (
            result + extended[lag_index : lag_index + total_rows] * weight[:, lag_index][None, :]
        )
    return silu(result)


def on_device(
    block_input,
    seq_pieces,
    norm_gain,
    w_zx,
    w_bc,
    w_dt,
    conv_x_weight,
    conv_x_bias,
    conv_bc_weight,
    conv_bc_bias,
    dt_bias,
    decay_rate,
    skip,
    gate_gain,
    w_out,
    cotangent,
):
    tok_rows, model_width = block_input.shape
    inner_own = w_zx.shape[2]
    heads_own = w_dt.shape[1]
    head_size = inner_own // heads_own
    edge_rows = conv_x_weight.shape[1] - 1
    inner_all = inner_own * lax.axis_size("head")
    width_own = model_width // lax.axis_size("head")
    hops = max(1, lax.axis_size("seq") // 4 - 1)
    first_core = lax.axis_index("head") == 0
    piece_index = lax.axis_index("seq")
    bounds = jnp.cumsum(seq_pieces)
    first_pieces = jnp.concatenate([jnp.zeros((1,), jnp.int32), bounds[:-1]])
    keep_own = 1.0 - jnp.any(first_pieces == piece_index).astype(F32)

    def own_half(values):
        return jnp.where(first_core, values[:, :width_own], values[:, width_own:])

    def far_half(values):
        return jnp.where(first_core, values[:, width_own:], values[:, :width_own])

    inputs32 = block_input.astype(F32)
    in_scale = lax.rsqrt(jnp.mean(inputs32 * inputs32, axis=-1, keepdims=True) + EPS)
    normed_bf = (inputs32 * in_scale * norm_gain).astype(BF16)
    w_x = w_zx[:, 1]
    dt_raw = mm(normed_bf, w_dt)
    bc_pre = mm(normed_bf, w_bc)
    x_pre = mm(normed_bf, w_x)
    conv_pre = jnp.concatenate([x_pre, bc_pre], axis=1)
    conv_weight = jnp.concatenate([conv_x_weight, conv_bc_weight], axis=0)
    conv_bias = jnp.concatenate([conv_x_bias, conv_bc_bias], axis=0)
    edge_prev = shifted(conv_pre[tok_rows - edge_rows :], 1) * keep_own
    activated, conv_pullback = jax.vjp(conv_act, conv_pre, edge_prev, conv_weight, conv_bias)
    x_flat = activated[:, :inner_own]
    bc_own = activated[:, inner_own:]
    bc_far = other_core(bc_own)
    b_mat = jnp.where(first_core, bc_own, bc_far)
    c_mat = jnp.where(first_core, bc_far, bc_own)

    shifted_raw = (dt_raw + dt_bias[None, :]).T
    step = jax.nn.softplus(shifted_raw)
    cumul = jnp.cumsum(-step * decay_rate[:, None], axis=1)
    level = cumul[:, -1]
    decay = jnp.exp(level)
    x_act = jnp.transpose(x_flat.reshape(tok_rows, heads_own, head_size), (1, 0, 2))
    x_step = x_act * step[:, :, None]
    tail = jnp.exp(level[:, None] - cumul)
    piece_state = jnp.einsum("hsp,sn->hpn", tail[:, :, None] * x_step, b_mat, precision=HIGH)
    w_late, normed_late, cot_late, piece_state = lax.optimization_barrier(
        (w_zx, normed_bf, cotangent, piece_state)
    )
    prefix = compose_from(decay * keep_own, piece_state, hops, 1)
    w_z = w_late[:, 0]
    gate_pre = mm(normed_late, w_z)
    cot_rows = own_first(cot_late, False)
    normed_rows = own_first(normed_late, False)
    normed_rows_late = own_first(normed_late, True)
    d_mixed = mm(cot_late, w_out.T)
    state_in = prefix * keep_own
    causal = (jnp.arange(tok_rows)[:, None] >= jnp.arange(tok_rows)[None, :])[None, :, :]
    scores = jnp.dot(c_mat, b_mat.T, precision=HIGH)
    spread = jnp.exp(jnp.where(causal, cumul[:, :, None] - cumul[:, None, :], -jnp.inf))
    weights = scores[None] * spread
    y_inside = jnp.einsum("hts,hsp->htp", weights, x_step, precision=HIGH)
    grown = jnp.exp(cumul)
    y_scan = y_inside + grown[:, :, None] * jnp.einsum(
        "tn,hpn->htp", c_mat, state_in, precision=HIGH
    )

    def flat(values):
        return jnp.transpose(values, (1, 0, 2)).reshape(tok_rows, inner_own)

    y_flat = flat(y_scan + skip[:, None, None] * x_act)
    sigma = jax.nn.sigmoid(gate_pre)
    z_silu = gate_pre * sigma
    gated = y_flat * z_silu
    d_hat = d_mixed * gate_gain[None, :]
    row_sums = jnp.stack([jnp.sum(gated * gated, axis=1), jnp.sum(d_hat * gated, axis=1)])
    row_sums = row_sums + other_core(row_sums)
    gate_scale = lax.rsqrt(row_sums[0] / inner_all + EPS)[:, None]
    gate_hat = gated * gate_scale
    row_dots = row_sums[1][:, None] * gate_scale
    mixed = (gate_hat * gate_gain[None, :]).astype(BF16)
    d_gated = gate_scale * (d_hat - gate_hat * (row_dots / inner_all))
    d_y_flat = d_gated * z_silu
    d_gate = (d_gated * y_flat * sigma * (1.0 + gate_pre * (1.0 - sigma))).astype(BF16)
    gate_gain_term = jnp.sum(d_mixed * gate_hat, axis=0)
    d_y = jnp.transpose(d_y_flat.reshape(tok_rows, heads_own, head_size), (1, 0, 2))

    d_y_grown = d_y * grown[:, :, None]
    d_state_local = jnp.einsum("htp,tn->hpn", d_y_grown, c_mat, precision=HIGH)
    grad_end = compose_from(decay * keep_own, d_state_local * keep_own, hops, -1)

    out_grad = scatter_sum(cot_rows, mixed, False).T
    z_grad = scatter_sum(normed_rows, d_gate, False)

    out_terms = mm(mixed, w_out)
    block_output = (
        own_half(inputs32) + (own_half(out_terms) + other_core(far_half(out_terms)))
    ).astype(BF16)

    skip_term = jnp.sum(d_y * x_act, axis=(1, 2))
    d_inside = jnp.einsum("hts,htp->hsp", weights, d_y, precision=HIGH)
    d_scores = jnp.sum(
        jnp.einsum("htp,hsp->hts", d_y, x_step, precision=HIGH) * spread, axis=0
    )
    d_c = jnp.dot(d_scores, b_mat, precision=HIGH) + jnp.einsum(
        "htp,hpn->tn", d_y_grown, state_in, precision=HIGH
    )
    d_b = jnp.dot(d_scores.T, c_mat, precision=HIGH)
    d_b = d_b + jnp.einsum("hsp,hpn->sn", tail[:, :, None] * x_step, grad_end, precision=HIGH)
    d_x_step = d_inside + tail[:, :, None] * jnp.einsum(
        "hpn,sn->hsp", grad_end, b_mat, precision=HIGH
    )
    d_step = jnp.sum(x_act * d_x_step, axis=2)
    d_cumul = jnp.sum(d_y * y_scan, axis=2) - step * d_step
    d_level = jnp.sum(grad_end * (decay[:, None, None] * state_in + piece_state), axis=(1, 2))
    d_cumul = d_cumul.at[:, -1].add(d_level)
    d_log = jnp.cumsum(d_cumul[:, ::-1], axis=1)[:, ::-1]
    rate_term = -jnp.sum(step * d_log, axis=1)
    d_raw = (d_step - decay_rate[:, None] * d_log) * jax.nn.sigmoid(shifted_raw)
    dt_bias_term = jnp.sum(d_raw, axis=1)
    d_x = flat(step[:, :, None] * d_x_step + skip[:, None, None] * d_y)

    bc_own_grad = jnp.where(first_core, d_b, d_c) + other_core(jnp.where(first_core, d_c, d_b))
    d_act = jnp.concatenate([d_x, bc_own_grad], axis=1)
    d_conv_pre, d_edge, conv_w_term, conv_b_term = conv_pullback(d_act)
    tail_grad = shifted(d_edge * keep_own, -1)
    d_conv_pre = jnp.concatenate(
        [d_conv_pre[: tok_rows - edge_rows], d_conv_pre[tok_rows - edge_rows :] + tail_grad], axis=0
    )
    d_x_pre = d_conv_pre[:, :inner_own].astype(BF16)
    d_bc = d_conv_pre[:, inner_own:].astype(BF16)
    d_dt = d_raw.T.astype(BF16)
    padded = jnp.pad(d_dt, ((0, 0), (0, -heads_own % 128)))
    early = inner_own * 3 // 4
    x_grad = jnp.concatenate(
        [
            scatter_sum(normed_rows, d_x_pre[:, :early], False),
            scatter_sum(
                normed_rows_late, jnp.concatenate([d_x_pre[:, early:], d_bc, padded], axis=1), True
            ),
        ],
        axis=1,
    )
    state_own = w_bc.shape[1]

    norm_terms = mm(d_gate, w_z.T)
    norm_terms = norm_terms + mm(d_x_pre, w_x.T)
    norm_terms = norm_terms + mm(d_bc, w_bc.T)
    norm_terms = norm_terms + mm(d_dt, w_dt.T)
    in_hat = inputs32 * in_scale
    row_dot = jnp.sum(norm_terms * norm_gain * in_hat, axis=1)
    row_dot = row_dot + other_core(row_dot)
    d_normed_own = own_half(norm_terms) + other_core(far_half(norm_terms))
    own_gain = jnp.where(first_core, norm_gain[:width_own], norm_gain[width_own:])
    own_hat = own_half(in_hat)
    input_grad = (
        in_scale * (d_normed_own * own_gain - own_hat * (row_dot[:, None] / model_width))
        + own_half(cotangent).astype(F32)
    )
    gain_own = jnp.sum(d_normed_own * own_hat, axis=0)

    terms = (
        gain_own,
        gate_gain_term,
        conv_w_term.T.reshape(-1),
        conv_b_term,
        dt_bias_term,
        rate_term,
        skip_term,
    )
    packed = total_sum(jnp.concatenate(terms))
    sums = []
    offset = 0
    for term in terms:
        sums.append(packed[offset : offset + term.shape[0]])
        offset += term.shape[0]
    conv_w = sums[2].reshape(edge_rows + 1, -1).T
    zx_grad = jnp.stack([z_grad, x_grad[:, :inner_own]], axis=1)
    return (
        block_output,
        input_grad,
        sums[0],
        zx_grad,
        x_grad[:, inner_own : inner_own + state_own],
        x_grad[:, inner_own + state_own : inner_own + state_own + heads_own],
        conv_w[:inner_own],
        sums[3][:inner_own],
        conv_w[inner_own:],
        sums[3][inner_own:],
        sums[4],
        sums[5],
        sums[6],
        sums[1],
        out_grad,
    )


def solution(mesh):
    placed = (
        P("seq", None),
        P(),
        P(),
        P(None, None, "head"),
        P(None, "head"),
        P(None, "head"),
        P("head", None),
        P("head"),
        P("head", None),
        P("head"),
        P("head"),
        P("head"),
        P("head"),
        P("head"),
        P("head", None),
        P("seq", None),
    )
    return jax.shard_map(
        on_device,
        mesh=mesh,
        in_specs=placed,
        out_specs=(
            P("seq", "head"),
            P("seq", "head"),
            P("head"),
            P("seq", None, "head"),
            P("seq", "head"),
            P("seq", "head"),
            P("head", None),
            P("head"),
            P("head", None),
            P("head"),
            P("head"),
            P("head"),
            P("head"),
            P("head"),
            P("head", "seq"),
        ),
        check_vma=False,
    )
```

```python
import jax
import jax.numpy as jnp
from jax import lax
from jax.sharding import PartitionSpec as P


EPS = 1e-05
HIGH = lax.Precision.HIGH
F32 = jnp.float32
BF16 = jnp.bfloat16


def shifted(value, steps):
    count = lax.axis_size("seq")
    initial, last = (max(0, -steps), min(count, count - steps))
    return lax.ppermute(value, "seq", [(s, s + steps) for s in range(initial, last)])


def other_core(value):
    return lax.ppermute(value, "head", [(0, 1), (1, 0)])


def bit_orders(count):
    bits = count.bit_length() - 1
    low = list(range(min(2, bits)))
    high = list(range(len(low), bits))
    return (low + high, low[::-1] + high)


def swap(value, phase):
    count = lax.axis_size("seq")
    orders = bit_orders(count)
    pairs = [
        (s * 2 + core, (s ^ (1 << orders[core][phase])) * 2 + core)
        for s in range(count)
        for core in range(2)
    ]
    return lax.ppermute(value, ("seq", "head"), pairs)


def own_first(matrix):
    count = lax.axis_size("seq")
    bits = count.bit_length() - 1
    width = matrix.shape[1]
    each = width // count
    masks = [
        [sum(((k >> (bits - 1 - i)) & 1) << order[i] for i in range(bits)) for k in range(count)]
        for order in bit_orders(count)
    ]
    mask = jnp.where(
        lax.axis_index("head") == 0,
        jnp.asarray(masks[0], jnp.int32),
        jnp.asarray(masks[1], jnp.int32),
    )
    source = (lax.axis_index("seq") ^ mask)[:, None] * each + jnp.arange(each)[None, :]
    chosen = (jnp.arange(width)[:, None] == source.reshape(1, width)).astype(BF16)
    return mm(matrix, chosen).astype(BF16)


def mm(a, b):
    return jnp.dot(a, b, preferred_element_type=F32)


def mm_rows(a, b):
    return lax.dot_general(a, b, (((0,), (0,)), ((), ())), preferred_element_type=F32)


def scatter_sum(left, right):
    count = lax.axis_size("seq")
    half = left.shape[1] // 2
    total = swap(mm_rows(left[:, half:], right), 0) + mm_rows(left[:, :half], right)
    for phase in range(1, count.bit_length() - 1):
        half = half // 2
        total = total[:half] + swap(total[half:], phase)
    return total


def total_sum(value):
    for phase in range(lax.axis_size("seq").bit_length() - 1):
        value = value + swap(value, phase)
    return value


def compose_from(decay, state, hops, sign):
    if hops <= 3:
        heads = decay.shape[0]
        row = jnp.zeros((1,) + state.shape[1:], F32)
        row = row + jnp.pad(decay, (0, state.shape[2] - heads))[None, None, :]
        packed = jnp.concatenate([state, row], axis=0)
        parts = []
        for k in range(1, hops + 1):
            parts.append(shifted(packed, sign * k))
        result = parts[-1][:heads]
        for part in parts[-2::-1]:
            result = part[:heads] + part[heads, 0, :heads][:, None, None] * result
        return result
    decay, state = (shifted(decay, sign), shifted(state, sign))
    reach = 1
    while reach < hops:
        far_decay, far_state = (shifted(decay, sign * reach), shifted(state, sign * reach))
        state = state + decay[:, None, None] * far_state
        decay = decay * far_decay
        reach *= 2
    return state


def silu(values):
    return values * jax.nn.sigmoid(values)


def conv_act(conv_pre, edge_prev, weight, bias):
    width_taps = weight.shape[1]
    total_rows = conv_pre.shape[0]
    extended = jnp.concatenate([edge_prev, conv_pre], axis=0)
    result = bias[None, :] + extended[0:total_rows] * weight[:, 0][None, :]
    for lag_index in range(1, width_taps):
        result = (
            result + extended[lag_index : lag_index + total_rows] * weight[:, lag_index][None, :]
        )
    return silu(result)


def on_device(
    block_input,
    seq_pieces,
    norm_gain,
    w_zx,
    w_bc,
    w_dt,
    conv_x_weight,
    conv_x_bias,
    conv_bc_weight,
    conv_bc_bias,
    dt_bias,
    decay_rate,
    skip,
    gate_gain,
    w_out,
    cotangent,
):
    tok_rows, model_width = block_input.shape
    inner_own = w_zx.shape[2]
    heads_own = w_dt.shape[1]
    head_size = inner_own // heads_own
    edge_rows = conv_x_weight.shape[1] - 1
    inner_all = inner_own * lax.axis_size("head")
    width_own = model_width // lax.axis_size("head")
    hops = max(1, lax.axis_size("seq") // 4 - 1)
    first_core = lax.axis_index("head") == 0
    piece_index = lax.axis_index("seq")
    bounds = jnp.cumsum(seq_pieces)
    first_pieces = jnp.concatenate([jnp.zeros((1,), jnp.int32), bounds[:-1]])
    keep_own = 1.0 - jnp.any(first_pieces == piece_index).astype(F32)

    def own_half(values):
        return jnp.where(first_core, values[:, :width_own], values[:, width_own:])

    def far_half(values):
        return jnp.where(first_core, values[:, width_own:], values[:, :width_own])

    inputs32 = block_input.astype(F32)
    in_scale = lax.rsqrt(jnp.mean(inputs32 * inputs32, axis=-1, keepdims=True) + EPS)
    normed_bf = (inputs32 * in_scale * norm_gain).astype(BF16)
    w_x = w_zx[:, 1]
    dt_raw = mm(normed_bf, w_dt)
    bc_pre = mm(normed_bf, w_bc)
    x_pre = mm(normed_bf, w_x)
    conv_pre = jnp.concatenate([x_pre, bc_pre], axis=1)
    conv_weight = jnp.concatenate([conv_x_weight, conv_bc_weight], axis=0)
    conv_bias = jnp.concatenate([conv_x_bias, conv_bc_bias], axis=0)
    edge_prev = shifted(conv_pre[tok_rows - edge_rows :], 1) * keep_own
    activated, conv_pullback = jax.vjp(conv_act, conv_pre, edge_prev, conv_weight, conv_bias)
    x_flat = activated[:, :inner_own]
    bc_own = activated[:, inner_own:]
    bc_far = other_core(bc_own)
    b_mat = jnp.where(first_core, bc_own, bc_far)
    c_mat = jnp.where(first_core, bc_far, bc_own)

    shifted_raw = (dt_raw + dt_bias[None, :]).T
    step = jax.nn.softplus(shifted_raw)
    cumul = jnp.cumsum(-step * decay_rate[:, None], axis=1)
    level = cumul[:, -1]
    decay = jnp.exp(level)
    x_act = jnp.transpose(x_flat.reshape(tok_rows, heads_own, head_size), (1, 0, 2))
    x_step = x_act * step[:, :, None]
    tail = jnp.exp(level[:, None] - cumul)
    piece_state = jnp.einsum("hsp,sn->hpn", tail[:, :, None] * x_step, b_mat, precision=HIGH)
    w_late, normed_late, cot_late, piece_state = lax.optimization_barrier(
        (w_zx, normed_bf, cotangent, piece_state)
    )
    prefix = compose_from(decay * keep_own, piece_state, hops, 1)
    w_z = w_late[:, 0]
    gate_pre = mm(normed_late, w_z)
    cot_rows = own_first(cot_late)
    normed_rows = own_first(normed_late)
    d_mixed = mm(cot_late, w_out.T)
    state_in = prefix * keep_own
    causal = (jnp.arange(tok_rows)[:, None] >= jnp.arange(tok_rows)[None, :])[None, :, :]
    scores = jnp.dot(c_mat, b_mat.T, precision=HIGH)
    spread = jnp.exp(jnp.where(causal, cumul[:, :, None] - cumul[:, None, :], -jnp.inf))
    weights = scores[None] * spread
    y_inside = jnp.einsum("hts,hsp->htp", weights, x_step, precision=HIGH)
    grown = jnp.exp(cumul)
    y_scan = y_inside + grown[:, :, None] * jnp.einsum(
        "tn,hpn->htp", c_mat, state_in, precision=HIGH
    )

    def flat(values):
        return jnp.transpose(values, (1, 0, 2)).reshape(tok_rows, inner_own)

    y_flat = flat(y_scan + skip[:, None, None] * x_act)
    sigma = jax.nn.sigmoid(gate_pre)
    z_silu = gate_pre * sigma
    gated = y_flat * z_silu
    d_hat = d_mixed * gate_gain[None, :]
    row_sums = jnp.stack([jnp.sum(gated * gated, axis=1), jnp.sum(d_hat * gated, axis=1)])
    row_sums = row_sums + other_core(row_sums)
    gate_scale = lax.rsqrt(row_sums[0] / inner_all + EPS)[:, None]
    gate_hat = gated * gate_scale
    row_dots = row_sums[1][:, None] * gate_scale
    mixed = (gate_hat * gate_gain[None, :]).astype(BF16)
    d_gated = gate_scale * (d_hat - gate_hat * (row_dots / inner_all))
    d_y_flat = d_gated * z_silu
    d_gate = (d_gated * y_flat * sigma * (1.0 + gate_pre * (1.0 - sigma))).astype(BF16)
    gate_gain_term = jnp.sum(d_mixed * gate_hat, axis=0)
    d_y = jnp.transpose(d_y_flat.reshape(tok_rows, heads_own, head_size), (1, 0, 2))

    d_y_grown = d_y * grown[:, :, None]
    d_state_local = jnp.einsum("htp,tn->hpn", d_y_grown, c_mat, precision=HIGH)
    grad_end = compose_from(decay * keep_own, d_state_local * keep_own, hops, -1)

    out_grad = scatter_sum(cot_rows, mixed).T
    z_grad = scatter_sum(normed_rows, d_gate)

    out_terms = mm(mixed, w_out)
    block_output = (
        own_half(inputs32) + (own_half(out_terms) + other_core(far_half(out_terms)))
    ).astype(BF16)

    skip_term = jnp.sum(d_y * x_act, axis=(1, 2))
    d_inside = jnp.einsum("hts,htp->hsp", weights, d_y, precision=HIGH)
    d_scores = jnp.sum(
        jnp.einsum("htp,hsp->hts", d_y, x_step, precision=HIGH) * spread, axis=0
    )
    d_c = jnp.dot(d_scores, b_mat, precision=HIGH) + jnp.einsum(
        "htp,hpn->tn", d_y_grown, state_in, precision=HIGH
    )
    d_b = jnp.dot(d_scores.T, c_mat, precision=HIGH)
    d_b = d_b + jnp.einsum("hsp,hpn->sn", tail[:, :, None] * x_step, grad_end, precision=HIGH)
    d_x_step = d_inside + tail[:, :, None] * jnp.einsum(
        "hpn,sn->hsp", grad_end, b_mat, precision=HIGH
    )
    d_step = jnp.sum(x_act * d_x_step, axis=2)
    d_cumul = jnp.sum(d_y * y_scan, axis=2) - step * d_step
    d_level = jnp.sum(grad_end * (decay[:, None, None] * state_in + piece_state), axis=(1, 2))
    d_cumul = d_cumul.at[:, -1].add(d_level)
    d_log = jnp.cumsum(d_cumul[:, ::-1], axis=1)[:, ::-1]
    rate_term = -jnp.sum(step * d_log, axis=1)
    d_raw = (d_step - decay_rate[:, None] * d_log) * jax.nn.sigmoid(shifted_raw)
    dt_bias_term = jnp.sum(d_raw, axis=1)
    d_x = flat(step[:, :, None] * d_x_step + skip[:, None, None] * d_y)

    bc_own_grad = jnp.where(first_core, d_b, d_c) + other_core(jnp.where(first_core, d_c, d_b))
    d_act = jnp.concatenate([d_x, bc_own_grad], axis=1)
    d_conv_pre, d_edge, conv_w_term, conv_b_term = conv_pullback(d_act)
    tail_grad = shifted(d_edge * keep_own, -1)
    d_conv_pre = jnp.concatenate(
        [d_conv_pre[: tok_rows - edge_rows], d_conv_pre[tok_rows - edge_rows :] + tail_grad], axis=0
    )
    d_x_pre = d_conv_pre[:, :inner_own].astype(BF16)
    d_bc = d_conv_pre[:, inner_own:].astype(BF16)
    d_dt = d_raw.T.astype(BF16)
    state_own = w_bc.shape[1]
    padded = jnp.pad(d_dt, ((0, 0), (0, -heads_own % 128)))
    early = (inner_own + state_own + padded.shape[1]) // 256 * 128
    x_grad = jnp.concatenate(
        [
            scatter_sum(normed_rows, d_x_pre[:, :early]),
            scatter_sum(normed_rows, jnp.concatenate([d_x_pre[:, early:], d_bc, padded], axis=1)),
        ],
        axis=1,
    )
    norm_terms = mm(d_gate, w_z.T)
    norm_terms = norm_terms + mm(d_x_pre, w_x.T)
    norm_terms = norm_terms + mm(d_bc, w_bc.T)
    norm_terms = norm_terms + mm(d_dt, w_dt.T)
    in_hat = inputs32 * in_scale
    row_dot = jnp.sum(norm_terms * norm_gain * in_hat, axis=1)
    row_dot = row_dot + other_core(row_dot)
    d_normed_own = own_half(norm_terms) + other_core(far_half(norm_terms))
    own_gain = jnp.where(first_core, norm_gain[:width_own], norm_gain[width_own:])
    own_hat = own_half(in_hat)
    input_grad = (
        in_scale * (d_normed_own * own_gain - own_hat * (row_dot[:, None] / model_width))
        + own_half(cotangent).astype(F32)
    )
    gain_own = jnp.sum(d_normed_own * own_hat, axis=0)

    terms = (
        gain_own,
        gate_gain_term,
        conv_w_term.T.reshape(-1),
        conv_b_term,
        dt_bias_term,
        rate_term,
        skip_term,
    )
    packed = total_sum(jnp.concatenate(terms))
    sums = []
    offset = 0
    for term in terms:
        sums.append(packed[offset : offset + term.shape[0]])
        offset += term.shape[0]
    conv_w = sums[2].reshape(edge_rows + 1, -1).T
    zx_grad = jnp.stack([z_grad, x_grad[:, :inner_own]], axis=1)
    return (
        block_output,
        input_grad,
        sums[0],
        zx_grad,
        x_grad[:, inner_own : inner_own + state_own],
        x_grad[:, inner_own + state_own : inner_own + state_own + heads_own],
        conv_w[:inner_own],
        sums[3][:inner_own],
        conv_w[inner_own:],
        sums[3][inner_own:],
        sums[4],
        sums[5],
        sums[6],
        sums[1],
        out_grad,
    )


def solution(mesh):
    placed = (
        P("seq", None),
        P(),
        P(),
        P(None, None, "head"),
        P(None, "head"),
        P(None, "head"),
        P("head", None),
        P("head"),
        P("head", None),
        P("head"),
        P("head"),
        P("head"),
        P("head"),
        P("head"),
        P("head", None),
        P("seq", None),
    )
    return jax.shard_map(
        on_device,
        mesh=mesh,
        in_specs=placed,
        out_specs=(
            P("seq", "head"),
            P("seq", "head"),
            P("head"),
            P("seq", None, "head"),
            P("seq", "head"),
            P("seq", "head"),
            P("head", None),
            P("head"),
            P("head", None),
            P("head"),
            P("head"),
            P("head"),
            P("head"),
            P("head"),
            P("head", "seq"),
        ),
        check_vma=False,
    )
```
